32 devices in a mesh: ctx: 16 (over z, y, x), tp: 2 (over core).
Axes of the slice: x: 2, y: 2, z: 4, core: 2. Of those that a mesh axis runs over, the one named last changes fastest.
Arguments:
- tokens: bfloat16 [2048, 2048], P('ctx'), may hold values from -6 to 6
- gain_attention: bfloat16 [2048], P('ctx'), may hold values from 0.5 to 1.5
- query_weight: bfloat16 [2048, 2048], P('ctx', 'tp'), may hold values from -0.125 to 0.125
- key_weight: bfloat16 [2048, 512], P('ctx', 'tp'), may hold values from -0.125 to 0.125
- value_weight: bfloat16 [2048, 512], P('ctx', 'tp'), may hold values from -0.125 to 0.125
- output_weight: bfloat16 [2048, 2048], P('ctx', 'tp'), may hold values from -3 to 3
- gain_feedforward: bfloat16 [2048], P('ctx'), may hold values from 0.5 to 1.5
- gate_weight: bfloat16 [2048, 8192], P('ctx', 'tp'), may hold values from -0.125 to 0.125
- up_weight: bfloat16 [2048, 8192], P('ctx', 'tp'), may hold values from -0.125 to 0.125
- down_weight: bfloat16 [2048, 8192], P('ctx', 'tp'), may hold values from -0.0625 to 0.0625
- cotangent: bfloat16 [2048, 2048], P('ctx'), may hold values from -6 to 6
Outputs:
- layer_output: float32 [2048, 2048], P('ctx')
- grad_tokens: float32 [2048, 2048], P('ctx')
- grad_gain_attention: float32 [2048], P('ctx')
- grad_query: float32 [2048, 2048], P('ctx', 'tp')
- grad_key: float32 [2048, 512], P('ctx', 'tp')
- grad_value: float32 [2048, 512], P('ctx', 'tp')
- grad_output_weight: float32 [2048, 2048], P('ctx', 'tp')
- grad_gain_feedforward: float32 [2048], P('ctx')
- grad_gate: float32 [2048, 8192], P('ctx', 'tp')
- grad_up: float32 [2048, 8192], P('ctx', 'tp')
- grad_down: float32 [2048, 8192], P('ctx', 'tp')
The draws below stay inside these ranges and needn't reach their ends.
All inputs are finite; a program needn't handle non-finite values.
Results may differ from the reference program's by a relative error of at most 0.018.
Values may be sent and summed in bfloat16 or wider, within the bound.
No kernel may reach another device: no remote copies, remote signals or barrier semaphores. Data moves between devices by JAX's collectives and lax.ppermute only.
A program may use at most 320 MiB of HBM per device.

```python
import math
import jax
import jax.numpy as jnp
from jax import lax

D = 2048
HEADS = 32
KV = 8
HD = 64
FF = 8192
BLK = 64
LEN = 2048
N_CTX = 16


def level_of(rng, extent, pieces, least, top_value):
    loudness, own = 1.0, jax.random.fold_in(rng, 6)
    for position, shards_of in pieces:
        heights = jnp.exp(jax.random.uniform(jax.random.fold_in(own, position), (shards_of,), jnp.float32, least / len(pieces), top_value / len(pieces)))
        loudness = loudness * jnp.repeat(heights, extent[position] // shards_of).reshape([-1 if axis == position else 1 for axis in range(len(extent))])
    return loudness


def bell_draw(own_key, extent, width, reach, cuts=(), kind=jnp.bfloat16):
    array = width * jax.random.normal(own_key, extent, jnp.float32)
    if cuts:
        array = array * level_of(own_key, extent, cuts, -0.22, 0.18)
    return jnp.clip(array, -reach, reach).astype(kind)


def setup_inputs(seed: int = 0) -> dict:
    seeds = jax.random.split(jax.random.key(seed), 12)
    tokens = bell_draw(seeds[0], (LEN, D), 1.0, 6.0, ((0, 16),))
    gain_attention = jnp.clip(1.0 + 0.1 * jax.random.normal(seeds[1], (D,), jnp.float32), 0.5, 1.5).astype(jnp.bfloat16)
    query_weight = bell_draw(seeds[2], (D, HEADS * HD), D ** -0.5, 0.125, ((0, 16), (1, 2)))
    key_weight = bell_draw(seeds[3], (D, KV * HD), D ** -0.5, 0.125, ((0, 16), (1, 2)))
    value_weight = bell_draw(seeds[4], (D, KV * HD), D ** -0.5, 0.125, ((0, 16), (1, 2)))
    output_weight = bell_draw(seeds[5], (D, HEADS * HD), 0.5, 3.0, ((0, 16), (1, 2)))
    gain_feedforward = jnp.clip(1.0 + 0.1 * jax.random.normal(seeds[6], (D,), jnp.float32), 0.5, 1.5).astype(jnp.bfloat16)
    gate_weight = bell_draw(seeds[7], (D, FF), D ** -0.5, 0.125, ((0, 16), (1, 2)))
    up_weight = bell_draw(seeds[8], (D, FF), D ** -0.5, 0.125, ((0, 16), (1, 2)))
    down_weight = bell_draw(seeds[9], (D, FF), FF ** -0.5, 0.0625, ((0, 16), (1, 2)))
    cotangent = bell_draw(seeds[10], (LEN, D), 1.0, 6.0, ((0, 16),))
    return dict(tokens=tokens, gain_attention=gain_attention, query_weight=query_weight, key_weight=key_weight, value_weight=value_weight, output_weight=output_weight, gain_feedforward=gain_feedforward, gate_weight=gate_weight, up_weight=up_weight, down_weight=down_weight, cotangent=cotangent)


@jax.custom_vjp
def low(v):
    return lax.optimization_barrier(v.astype(jnp.bfloat16)).astype(jnp.float32)

@jax.custom_vjp
def low_back(v):
    return v

def low_keep(v):
    return (low(v), None)

def low_pass(kept, grad):
    return (grad,)

def back_keep(v):
    return (v, None)

def back_low(kept, grad):
    return (low(grad),)
low.defvjp(low_keep, low_pass)
low_back.defvjp(back_keep, back_low)

def precise(left_side, right_side):
    return jnp.dot(left_side, right_side, precision=lax.Precision.HIGHEST, preferred_element_type=jnp.float32)

def token_positions(total_rows):
    row_index = jnp.arange(total_rows, dtype=jnp.int32)
    shard_index = row_index // (2 * BLK)
    within = row_index % (2 * BLK)
    return jnp.where(within < BLK, shard_index * BLK + within, (2 * N_CTX - 1 - shard_index) * BLK + within - BLK)

def rope_tables(positions):
    frequency = jnp.exp(-jnp.arange(HD // 2, dtype=jnp.float32) * (2.0 * math.log(500000.0) / HD))
    angles = positions.astype(jnp.float32)[:, None] * frequency[None, :]
    return (jnp.cos(angles), jnp.sin(angles))

def rotate(values, cosine, sine_part):
    front_half = values[..., :HD // 2]
    back_half = values[..., HD // 2:]
    cosine = cosine[:, None, :]
    sine_part = sine_part[:, None, :]
    return jnp.concatenate([front_half * cosine - back_half * sine_part, back_half * cosine + front_half * sine_part], axis=-1)

def rms_normed(values, gain_vec):
    inverse = lax.rsqrt(lax.optimization_barrier(jnp.mean(values * values, axis=-1, keepdims=True)) + 1e-05)
    return values * inverse * gain_vec

def attention(queries, keys_rot, values_in, positions):
    total_rows = queries.shape[0]
    block_rows = math.gcd(512, total_rows)
    groups = HEADS // KV
    grouped = queries.reshape(total_rows // block_rows, block_rows, KV, groups, HD)
    query_pos = positions.reshape(total_rows // block_rows, block_rows)
    score_scale = 1.0 / math.sqrt(HD)

    def one_block(pair_in):
        query_block, pos_block = pair_in
        scores = jnp.einsum('qkgd,tkd->kgqt', query_block, keys_rot, precision=lax.Precision.HIGHEST) * score_scale
        scores = low_back(scores)
        visible = positions[None, None, None, :] <= pos_block[None, None, :, None]
        scores = jnp.where(visible, scores, -jnp.inf)
        maxima = lax.optimization_barrier(jnp.max(scores, axis=-1, keepdims=True))
        exps_all = jnp.exp(scores - maxima)
        weights = exps_all / lax.optimization_barrier(jnp.sum(exps_all, axis=-1, keepdims=True))
        mixed_block = jnp.einsum('kgqt,tkd->qkgd', low(weights), values_in, precision=lax.Precision.HIGHEST)
        return mixed_block.reshape(block_rows, HEADS * HD)
    outputs = lax.map(jax.checkpoint(one_block), (grouped, query_pos))
    return outputs.reshape(total_rows, HEADS * HD)

def layer(tokens, gain_attention, query_weight, key_weight, value_weight, output_weight, gain_feedforward, gate_weight, up_weight, down_weight):
    total_rows = tokens.shape[0]
    positions = token_positions(total_rows)
    cosine, sine_part = rope_tables(positions)
    normed = low(rms_normed(tokens, gain_attention))
    queries = low_back(precise(normed, query_weight)).reshape(total_rows, HEADS, HD)
    queries = low(rotate(queries, cosine, sine_part))
    keys_rot = low_back(precise(normed, key_weight)).reshape(total_rows, KV, HD)
    keys_rot = low(rotate(keys_rot, cosine, sine_part))
    values_in = low(low_back(precise(normed, value_weight))).reshape(total_rows, KV, HD)
    mixed_heads = low(low_back(attention(queries, keys_rot, values_in, positions)))
    branch = low_back(precise(mixed_heads, output_weight.T))
    middle = tokens + branch
    normed_ff = low(rms_normed(middle, gain_feedforward))
    gate_pre = low_back(precise(normed_ff, gate_weight))
    upward = low_back(precise(normed_ff, up_weight))
    hidden = low(jax.nn.silu(gate_pre) * upward)
    return middle + precise(hidden, down_weight.T)

def reference(tokens, gain_attention, query_weight, key_weight, value_weight, output_weight, gain_feedforward, gate_weight, up_weight, down_weight, cotangent):
    floats = [item.astype(jnp.float32) for item in (tokens, gain_attention, query_weight, key_weight, value_weight, output_weight, gain_feedforward, gate_weight, up_weight, down_weight)]
    layer_output, pullback = jax.vjp(layer, *floats)
    grads = pullback(cotangent.astype(jnp.float32))
    return (layer_output, grads[0], grads[1], grads[2], grads[3], grads[4], grads[5], grads[6], grads[7], grads[8], grads[9])
```

```python
import functools
import math

import jax
import jax.numpy as jnp
from jax import lax
from jax.experimental import pallas as pl
from jax.experimental.pallas import tpu as pltpu
from jax.sharding import PartitionSpec as P

HD = 64
EPSILON = 1e-05
BF = jnp.bfloat16
F32 = jnp.float32
TK = 512
NEG = -1e30


def mm(left_side, right_side):
    return jnp.dot(left_side, right_side, preferred_element_type=F32)


def mm_nt(left_side, right_side):
    return lax.dot_general(
        left_side, right_side, (((1,), (1,)), ((), ())), preferred_element_type=F32
    )


def mm_tn(left_side, right_side):
    return lax.dot_general(
        left_side, right_side, (((0,), (0,)), ((), ())), preferred_element_type=F32
    )


def rotated(values, cosine, sine_part):
    lane = lax.broadcasted_iota(jnp.int32, values.shape, 1) % 64
    swapped = jnp.where(lane < 32, pltpu.roll(values, 96, 1), pltpu.roll(values, 32, 1))
    return values * cosine + swapped * sine_part


def rope_forward_kernel(groups, qkv_ref, scale_ref, cos_ref, sin_ref, q_ref, kv_ref):
    rows = qkv_ref.shape[0]
    scale = scale_ref[...]
    cosine, sine_part = cos_ref[...], sin_ref[...]
    lane = lax.broadcasted_iota(jnp.int32, (rows, 128), 1)
    for head in range(groups):
        part = qkv_ref[:, (head // 2) * 128 : (head // 2) * 128 + 128] * scale
        if head % 2:
            part = pltpu.roll(part, 64, 1)
        turned = rotated(part, cosine, sine_part)
        turned = jnp.where(lane < 64, turned.astype(BF).astype(F32) * (1.0 / math.sqrt(HD)), 0.0)
        q_ref[:, head] = turned.astype(BF).reshape(rows // 64, 64, 128)
    part = qkv_ref[:, groups * 64 : groups * 64 + 128] * scale
    kv_ref[...] = rotated(part, cosine, sine_part).astype(BF)


def rope_backward_kernel(groups, pieces, *refs):
    dq_ref, dkv_refs, (scale_ref, cos_ref, sin_ref, out_ref) = (
        refs[0],
        refs[1 : 1 + pieces],
        refs[1 + pieces :],
    )
    rows = out_ref.shape[0]
    scale = scale_ref[...]
    cosine, sine_part = cos_ref[...], -sin_ref[...]
    lane = lax.broadcasted_iota(jnp.int32, (rows, 128), 1)
    for pair in range(groups // 2):
        first = rotated(dq_ref[:, 2 * pair].reshape(rows, 128), cosine, sine_part)
        second = rotated(dq_ref[:, 2 * pair + 1].reshape(rows, 128), cosine, sine_part)
        both = jnp.where(lane < 64, first, pltpu.roll(second, 64, 1))
        out_ref[:, pair * 128 : pair * 128 + 128] = (
            both * (scale * (1.0 / math.sqrt(HD)))
        ).astype(BF)
    total = dkv_refs[0][...].astype(F32)
    for ref in dkv_refs[1:]:
        total = total + ref[...].astype(F32)
    out_ref[:, groups * 64 : groups * 64 + 128] = (
        rotated(total, cosine, sine_part) * scale
    ).astype(BF)


def sort_keys(pbk_ref, kv_ref, sorted_ref):
    for block in range(kv_ref.shape[0] // 64):
        at = pl.multiple_of(pbk_ref[block] * 64, 64)
        sorted_ref[pl.ds(at, 64), :] = kv_ref[block * 64 : block * 64 + 64, :]


def visible(tile_index, block_pos, rows):
    key_pos = tile_index * TK + lax.broadcasted_iota(jnp.int32, (rows, TK), 1)
    query_pos = block_pos * 64 + lax.broadcasted_iota(jnp.int32, (rows, TK), 0) % 64
    return key_pos <= query_pos


def attention_forward_kernel(
    groups, pbq_ref, pbk_ref, q_ref, kv_ref, mixed_ref, aux_ref, sorted_ref, score_ref
):
    step = pl.program_id(0)
    rows = groups * 64

    @pl.when(step == 0)
    def _():
        sort_keys(pbk_ref, kv_ref, sorted_ref)

    block_pos = pbq_ref[step]
    tiles = (block_pos * 64) // TK + 1
    queries = q_ref[0].reshape(rows, 128)

    def first_pass(tile_index, maxima):
        keys = sorted_ref[pl.ds(pl.multiple_of(tile_index * TK, TK), TK), :]
        scores = mm_nt(queries, keys)
        scores = jnp.where(visible(tile_index, block_pos, rows), scores, NEG)
        score_ref[tile_index] = scores
        for part in range(TK // 128):
            maxima = jnp.maximum(maxima, scores[:, part * 128 : part * 128 + 128])
        return maxima

    maxima = lax.fori_loop(0, tiles, first_pass, jnp.full((rows, 128), NEG, F32))
    row_max = jnp.max(maxima, axis=1, keepdims=True)

    def second_pass(tile_index, carry):
        totals, accum = carry
        keys = sorted_ref[pl.ds(pl.multiple_of(tile_index * TK, TK), TK), :]
        weights = jnp.exp(score_ref[tile_index] - row_max)
        for part in range(TK // 128):
            totals = totals + weights[:, part * 128 : part * 128 + 128]
        return totals, accum + mm(weights.astype(BF), keys)

    zeros = jnp.zeros((rows, 128), F32)
    totals, accum = lax.fori_loop(0, tiles, second_pass, (zeros, zeros))
    row_total = jnp.sum(totals, axis=1, keepdims=True)
    accum = accum * (1.0 / row_total)
    lane = lax.broadcasted_iota(jnp.int32, (rows, 128), 1)
    aux_ref[0] = jnp.where(lane < 64, row_max + jnp.log(row_total), accum)
    short = lax.broadcasted_iota(jnp.int32, (64, 128), 1)
    for pair in range(groups // 2):
        first = accum[2 * pair * 64 : 2 * pair * 64 + 64]
        second = accum[(2 * pair + 1) * 64 : (2 * pair + 1) * 64 + 64]
        mixed_ref[:, pair * 128 : pair * 128 + 128] = jnp.where(
            short < 64, pltpu.roll(first, 64, 1), second
        ).astype(BF)


def attention_backward_kernel(
    groups, pbq_ref, pbk_ref, q_ref, g_ref, aux_ref, kv_ref, dq_ref, dkv_ref, sorted_ref, sum_ref
):
    step = pl.program_id(0)
    rows = groups * 64

    @pl.when(step == 0)
    def _():
        sort_keys(pbk_ref, kv_ref, sorted_ref)
        sum_ref[...] = jnp.zeros(sum_ref.shape, F32)

    block_pos = pbq_ref[step]
    tiles = (block_pos * 64) // TK + 1
    queries = q_ref[0].reshape(rows, 128)
    aux = aux_ref[0]
    short = lax.broadcasted_iota(jnp.int32, (64, 128), 1)
    parts = []
    for head in range(groups):
        part = g_ref[:, (head // 2) * 128 : (head // 2) * 128 + 128].astype(F32)
        if head % 2 == 0:
            part = pltpu.roll(part, 64, 1)
        parts.append(jnp.where(short < 64, 0.0, part))
    grads_f = jnp.concatenate(parts, axis=0)
    delta = jnp.sum(grads_f * aux, axis=1, keepdims=True)
    log_total = aux[:, :1]
    grads = grads_f.astype(BF)

    def visit(tile_index, grad_q):
        where_at = pl.ds(pl.multiple_of(tile_index * TK, TK), TK)
        keys = sorted_ref[where_at, :]
        scores = mm_nt(queries, keys)
        scores = jnp.where(visible(tile_index, block_pos, rows), scores - log_total, NEG)
        weights = jnp.exp(scores)
        grad_prob = mm_nt(grads, keys)
        grad_score = (weights * (grad_prob - delta)).astype(BF)
        sum_ref[where_at, :] += mm_tn(grad_score, queries) + mm_tn(weights.astype(BF), grads)
        return grad_q + mm(grad_score, keys)

    grad_q = lax.fori_loop(0, tiles, visit, jnp.zeros((rows, 128), F32))
    dq_ref[0] = grad_q.reshape(groups, 64, 128)

    @pl.when(step == pl.num_programs(0) - 1)
    def _():
        for block in range(dkv_ref.shape[0] // 64):
            at = pl.multiple_of(pbk_ref[block] * 64, 64)
            dkv_ref[block * 64 : block * 64 + 64, :] = sum_ref[pl.ds(at, 64), :].astype(BF)


def rope_forward(qkv, scale, cosine, sine_part, groups):
    rows = qkv.shape[0]
    return pl.pallas_call(
        functools.partial(rope_forward_kernel, groups),
        out_shape=(
            jax.ShapeDtypeStruct((rows // 64, groups, 64, 128), BF),
            jax.ShapeDtypeStruct((rows, 128), BF),
        ),
        name="rope_forward",
    )(qkv, scale, cosine, sine_part)


def rope_backward(dq, dkv_pieces, scale, cosine, sine_part, groups):
    rows = scale.shape[0]
    return pl.pallas_call(
        functools.partial(rope_backward_kernel, groups, len(dkv_pieces)),
        out_shape=jax.ShapeDtypeStruct((rows, groups * 64 + 128), BF),
        name="rope_backward",
    )(dq, *dkv_pieces, scale, cosine, sine_part)


def attention_forward(queries, kv, pbq, pbk):
    blocks, groups = queries.shape[:2]
    keys = kv.shape[0]
    smem = pl.BlockSpec(memory_space=pltpu.SMEM)
    return pl.pallas_call(
        functools.partial(attention_forward_kernel, groups),
        grid=(blocks,),
        in_specs=[
            smem,
            smem,
            pl.BlockSpec((1, groups, 64, 128), lambda i: (i, 0, 0, 0)),
            pl.BlockSpec((keys, 128), lambda i: (0, 0)),
        ],
        out_specs=(
            pl.BlockSpec((64, groups * 64), lambda i: (i, 0)),
            pl.BlockSpec((1, groups * 64, 128), lambda i: (i, 0, 0)),
        ),
        out_shape=(
            jax.ShapeDtypeStruct((blocks * 64, groups * 64), BF),
            jax.ShapeDtypeStruct((blocks, groups * 64, 128), F32),
        ),
        scratch_shapes=[
            pltpu.VMEM((keys, 128), BF),
            pltpu.VMEM((keys // TK, groups * 64, TK), F32),
        ],
        name="attention_forward",
    )(pbq, pbk, queries, kv)


def attention_backward(queries, grads, aux, kv, pbq, pbk):
    blocks, groups = queries.shape[:2]
    keys = kv.shape[0]
    smem = pl.BlockSpec(memory_space=pltpu.SMEM)
    return pl.pallas_call(
        functools.partial(attention_backward_kernel, groups),
        grid=(blocks,),
        in_specs=[
            smem,
            smem,
            pl.BlockSpec((1, groups, 64, 128), lambda i: (i, 0, 0, 0)),
            pl.BlockSpec((64, groups * 64), lambda i: (i, 0)),
            pl.BlockSpec((1, groups * 64, 128), lambda i: (i, 0, 0)),
            pl.BlockSpec((keys, 128), lambda i: (0, 0)),
        ],
        out_specs=(
            pl.BlockSpec((1, groups, 64, 128), lambda i: (i, 0, 0, 0)),
            pl.BlockSpec((keys, 128), lambda i: (0, 0)),
        ),
        out_shape=(
            jax.ShapeDtypeStruct((blocks, groups, 64, 128), F32),
            jax.ShapeDtypeStruct((keys, 128), BF),
        ),
        scratch_shapes=[pltpu.VMEM((keys, 128), BF), pltpu.VMEM((keys, 128), F32)],
        name="attention_backward",
    )(pbq, pbk, queries, grads, aux, kv)


def per_device(
    tokens,
    gain_attention,
    query_weight,
    key_weight,
    value_weight,
    output_weight,
    gain_feedforward,
    gate_weight,
    up_weight,
    down_weight,
    cotangent,
):
    shard_rows, width = tokens.shape
    n_ctx = lax.axis_size("ctx")
    ctx_index = lax.axis_index("ctx")
    core = lax.axis_index("tp")
    na = key_weight.shape[1] // HD
    nb = n_ctx // na
    a_index, b_index = ctx_index // nb, ctx_index % nb
    d_rows = width // n_ctx
    half = width // 2
    group_rows = na * shard_rows
    groups = query_weight.shape[1] // key_weight.shape[1]
    bits = nb.bit_length() - 1

    def shift_a(value, k):
        pairs = [(i, ((i // nb + k) % na) * nb + i % nb) for i in range(n_ctx)]
        return lax.ppermute(value, "ctx", pairs)

    def swap_b(value, m):
        return lax.ppermute(value, "ctx", [(i, (i // nb) * nb + ((i % nb) ^ m)) for i in range(n_ctx)])

    def swap_core(value):
        return lax.ppermute(value, "tp", [(0, 1), (1, 0)])

    def both_cores(own, other, axis):
        first = jnp.where(core == 0, own, other)
        second = jnp.where(core == 0, other, own)
        return jnp.concatenate([first, second], axis=axis)

    def feature_blocks(value, ms):
        blocked = value.reshape(shard_rows, na, nb, d_rows)
        return jnp.concatenate(
            [
                lax.dynamic_slice_in_dim(blocked, b_index ^ m, 1, 2).reshape(
                    shard_rows, na * d_rows
                )
                for m in ms
            ],
            axis=1,
        )

    def half_features(value):
        return feature_blocks(value, [core * (nb // 2) + j for j in range(nb // 2)])

    def natural_features(value):
        stacked = value.reshape(shard_rows, nb, na, d_rows)
        return jnp.concatenate(
            [
                lax.dynamic_slice_in_dim(stacked, b_index ^ j, 1, 1).reshape(
                    shard_rows, na, 1, d_rows
                )
                for j in range(nb)
            ],
            axis=2,
        ).reshape(shard_rows, width)

    def gather_rows(own_half):
        pieces = [own_half] + [shift_a(own_half, k) for k in range(1, na)]
        stacked = jnp.concatenate(pieces, axis=0)
        return both_cores(stacked, swap_core(stacked), 1)

    def reduce_rows(product_of_half):
        other = swap_core(product_of_half(1 - core).astype(BF))
        total = product_of_half(core) + other.astype(F32)
        sent = total.astype(BF).reshape(na, shard_rows, half)
        result = total[:shard_rows]
        for k in range(1, na):
            result = result + shift_a(sent[k], na - k).astype(F32)
        return result

    def half_rows(value, which):
        return lax.dynamic_slice_in_dim(value, which * half, half, 0)

    def gather_weight(blocks):
        first = blocks(a_index)
        pieces = [first] + [shift_a(blocks((a_index + k) % na), k) for k in range(1, na)]
        stacked = jnp.zeros((na,) + first.shape, first.dtype)
        for k in range(na):
            stacked = lax.dynamic_update_slice_in_dim(
                stacked, pieces[k][None], (a_index - k) % na, 0
            )
        own = stacked.reshape(na * d_rows, first.shape[1])
        if bits != 2:
            return jnp.concatenate([own] + [swap_b(own, m) for m in range(1, nb)], axis=0)
        split = own.shape[0] // 2
        from_one, from_two = swap_b(own, 1), swap_b(own, 2)
        from_three = [swap_b(from_one[:split], 2), swap_b(from_two[split:], 1)]
        return jnp.concatenate([own, from_one, from_two] + from_three, axis=0)

    def scatter_grad(grad, out_columns):
        columns = grad.shape[1]
        chunk = na * d_rows
        sent = grad.astype(BF).reshape(nb, chunk, columns)
        own = grad[:chunk]
        if bits != 2:
            for m in range(1, nb):
                own = own + swap_b(sent[m], m).astype(F32)
        else:
            split = chunk // 2
            parts = []
            for rows, m, n in ((slice(0, split), 1, 2), (slice(split, chunk), 2, 1)):
                far = grad[n * chunk : (n + 1) * chunk][rows]
                far = far + swap_b(sent[3][rows], m).astype(F32)
                near = own[rows] + swap_b(sent[m][rows], m).astype(F32)
                parts.append(near + swap_b(far.astype(BF), n).astype(F32))
            own = jnp.concatenate(parts, axis=0)
        blocks = own.astype(BF).reshape(na, d_rows, columns)
        pieces = []
        for k in range(na):
            piece = lax.dynamic_slice_in_dim(blocks, (a_index - k) % na, 1, 0)[0]
            pieces.append(piece if k == 0 else shift_a(piece, na - k))
        outs = []
        at = 0
        for size in out_columns:
            out = jnp.zeros((d_rows, na, size), F32)
            for k in range(na):
                part = pieces[k][:, at : at + size].astype(F32)
                out = lax.dynamic_update_slice_in_dim(
                    out, part[:, None], (a_index + k) % na, 1
                )
            outs.append(out.reshape(d_rows, na * size))
            at += size
        return outs

    def unit_block(weight, which):
        size = weight.shape[1] // na
        return lax.dynamic_slice_in_dim(weight, which * size, size, 1)

    gain_a = gain_attention.astype(F32)[:, None]
    gain_m = gain_feedforward.astype(F32)[:, None]

    def gained(weight, gain):
        return (weight.astype(F32) * gain).astype(BF)

    def qkv_blocks(which):
        return jnp.concatenate(
            [
                gained(unit_block(weight, which), gain_a)
                for weight in (query_weight, key_weight, value_weight)
            ],
            axis=1,
        )

    qkv_all = gather_weight(qkv_blocks)
    x_half = half_features(tokens)
    x_all = gather_rows(x_half)
    output_all = gather_weight(lambda which: unit_block(output_weight, which))
    gate_all = gather_weight(lambda which: gained(unit_block(gate_weight, which), gain_m))
    up_all = gather_weight(lambda which: gained(unit_block(up_weight, which), gain_m))
    down_all = gather_weight(lambda which: unit_block(down_weight, which))
    c_half = half_features(cotangent)
    c_all = gather_rows(c_half)

    k_shards = ((a_index - jnp.arange(na, dtype=jnp.int32)) % na) * nb + b_index
    pbq = jnp.stack([k_shards, 2 * n_ctx - 1 - k_shards], axis=1).reshape(na * 2)
    m_shards = (
        ((a_index - jnp.arange(na, dtype=jnp.int32)) % na)[None, :] * nb
        + (b_index ^ jnp.arange(nb, dtype=jnp.int32))[:, None]
    )
    pbk = jnp.stack([m_shards, 2 * n_ctx - 1 - m_shards], axis=2).reshape(nb * na * 2)
    block_rows = shard_rows // 2
    positions = (
        pbq[:, None] * block_rows + jnp.arange(block_rows, dtype=jnp.int32)[None, :]
    ).reshape(group_rows)
    frequency = jnp.exp(
        -jnp.arange(HD // 2, dtype=F32) * (2.0 * math.log(500000.0) / HD)
    )
    angles = positions.astype(F32)[:, None] * frequency[None, :]
    cos_part, sin_part = jnp.cos(angles), jnp.sin(angles)
    cosine = jnp.concatenate([cos_part, cos_part, jnp.ones((group_rows, HD), F32)], axis=1)
    sine_part = jnp.concatenate([-sin_part, sin_part, jnp.zeros((group_rows, HD), F32)], axis=1)

    x_f = x_all.astype(F32)
    r1 = lax.rsqrt(jnp.mean(x_f * x_f, axis=1, keepdims=True) + EPSILON)
    qkv = mm(x_all, qkv_all)
    queries, kv_own = rope_forward(qkv, r1, cosine, sine_part, groups)
    kv = jnp.concatenate([kv_own] + [swap_b(kv_own, m) for m in range(1, nb)], axis=0)
    mixed, aux = attention_forward(queries, kv, pbq, pbk)
    branch = reduce_rows(lambda which: mm_nt(mixed, half_rows(output_all, which)))
    middle = x_half.astype(F32) + branch

    middle_all = gather_rows(middle.astype(BF))
    middle_f = middle_all.astype(F32)
    r2 = lax.rsqrt(jnp.mean(middle_f * middle_f, axis=1, keepdims=True) + EPSILON)
    gate_pre = mm(middle_all, gate_all) * r2
    upward = mm(middle_all, up_all) * r2
    sigmoid_gate = jax.nn.sigmoid(gate_pre)
    silu_gate = gate_pre * sigmoid_gate
    hidden = (silu_gate * upward).astype(BF)

    grad_hidden = mm(c_all, down_all)
    grad_gate_pre = (
        grad_hidden * upward * sigmoid_gate * (1.0 + gate_pre * (1.0 - sigmoid_gate)) * r2
    ).astype(BF)
    grad_upward = (grad_hidden * silu_gate * r2).astype(BF)
    grad_ff = reduce_rows(
        lambda which: mm_nt(grad_gate_pre, half_rows(gate_all, which))
        + mm_nt(grad_upward, half_rows(up_all, which))
    )

    def norm_backward(values, inverse, grad_scaled):
        part = jnp.sum(grad_scaled * values, axis=1)
        mean = ((part + swap_core(part)) * (1.0 / width))[:, None]
        return grad_scaled - values * (inverse * inverse) * mean

    grad_middle = c_half.astype(F32) + norm_backward(middle, r2[:shard_rows], grad_ff)
    branch_all = gather_rows(grad_middle.astype(BF))

    grad_mixed = mm(branch_all, output_all).astype(BF)
    dq, dkv = attention_backward(queries, grad_mixed, aux, kv, pbq, pbk)
    dkv = dkv.reshape(nb, group_rows, 2 * HD)
    dkv_pieces = [dkv[0]] + [swap_b(dkv[m], m) for m in range(1, nb)]
    grad_qkv = rope_backward(dq, dkv_pieces, r1, cosine, sine_part, groups)
    grad_in = reduce_rows(lambda which: mm_nt(grad_qkv, half_rows(qkv_all, which)))
    grad_tokens = grad_middle + norm_backward(x_half.astype(F32), r1[:shard_rows], grad_in)

    ff_out = reduce_rows(lambda which: mm_nt(hidden, half_rows(down_all, which)))

    def whole_rows(value):
        return natural_features(both_cores(value, swap_core(value), 1))

    layer_output = whole_rows(middle + ff_out)
    grad_tokens = whole_rows(grad_tokens)

    units = gate_all.shape[1]
    (grad_down,) = scatter_grad(mm_tn(c_all, hidden), [units])
    (grad_gate,) = scatter_grad(mm_tn(middle_all, grad_gate_pre), [units])
    (grad_up,) = scatter_grad(mm_tn(middle_all, grad_upward), [units])
    (grad_output,) = scatter_grad(mm_tn(branch_all, mixed), [groups * HD])
    grad_query, grad_key, grad_value = scatter_grad(
        mm_tn(x_all, grad_qkv), [groups * HD, HD, HD]
    )

    def weight_dot(weight, grad):
        return jnp.sum(weight.astype(F32) * grad, axis=1)

    part_a = (
        weight_dot(query_weight, grad_query)
        + weight_dot(key_weight, grad_key)
        + weight_dot(value_weight, grad_value)
    )
    part_m = weight_dot(gate_weight, grad_gate) + weight_dot(up_weight, grad_up)
    return (
        layer_output,
        grad_tokens,
        part_a + swap_core(part_a),
        grad_query * gain_a,
        grad_key * gain_a,
        grad_value * gain_a,
        grad_output,
        part_m + swap_core(part_m),
        grad_gate * gain_m,
        grad_up * gain_m,
        grad_down,
    )


def solution(mesh):
    rows, units = P("ctx", None), P("ctx", "tp")
    in_specs = (rows, P("ctx"), units, units, units, units, P("ctx"), units, units, units, rows)
    out_specs = (rows, rows, P("ctx"), units, units, units, units, P("ctx"), units, units, units)
    return jax.shard_map(
        per_device, mesh=mesh, in_specs=in_specs, out_specs=out_specs, check_vma=False
    )
```

```python
import functools
import math

import jax
import jax.numpy as jnp
from jax import lax
from jax.experimental import pallas as pl
from jax.experimental.pallas import tpu as pltpu
from jax.sharding import PartitionSpec as P


HD = 64
EPSILON = 1e-05
BF = jnp.bfloat16
F32 = jnp.float32
TK = 512
NEG = -1e30


def mm(left_side, right_side):
    return jnp.dot(left_side, right_side, preferred_element_type=F32)


def mm_nt(left_side, right_side):
    return lax.dot_general(
        left_side, right_side, (((1,), (1,)), ((), ())), preferred_element_type=F32
    )


def mm_tn(left_side, right_side):
    return lax.dot_general(
        left_side, right_side, (((0,), (0,)), ((), ())), preferred_element_type=F32
    )


def finish_kernel(sizes, dots, na, *refs):
    index_ref, pieces, gain_ref = refs[0], refs[1 : 1 + na], refs[1 + na]
    weights = refs[2 + na : 2 + na + (len(sizes) if dots else 0)]
    outs = refs[2 + na + len(weights) : 2 + na + len(weights) + len(sizes)]
    rest = refs[2 + na + len(weights) + len(sizes) :]
    stacked_ref = rest[-1]
    for k in range(na):
        stacked_ref[index_ref[0] ^ k] = pieces[k][...]
    gain = gain_ref[...]
    total = jnp.zeros(gain.shape, F32)
    at = 0
    for n, size in enumerate(sizes):
        for block in range(na):
            part = stacked_ref[block][:, at : at + size].astype(F32)
            where_to = slice(block * size, block * size + size)
            if dots:
                total = total + jnp.sum(
                    part * weights[n][:, where_to].astype(F32), axis=1, keepdims=True
                )
                part = part * gain
            outs[n][:, where_to] = part
        at += size
    if dots:
        rest[0][...] = total


def finish(index, pieces, gain, weights, sizes):
    na = len(pieces)
    rows, columns = pieces[0].shape
    smem = pl.BlockSpec(memory_space=pltpu.SMEM)
    vmem = pl.BlockSpec(memory_space=pltpu.VMEM)
    shapes = [jax.ShapeDtypeStruct((rows, na * size), F32) for size in sizes]
    if weights:
        shapes.append(jax.ShapeDtypeStruct((rows, 1), F32))
    return pl.pallas_call(
        functools.partial(finish_kernel, tuple(sizes), bool(weights), na),
        in_specs=[smem] + [vmem] * (na + 1 + len(weights)),
        out_specs=[vmem] * len(shapes),
        out_shape=shapes,
        scratch_shapes=[pltpu.VMEM((na, rows, columns), BF)],
        name="finish",
    )(index, *pieces, gain, *weights)


def rotated(values, cosine, sine_part):
    lane = lax.broadcasted_iota(jnp.int32, values.shape, 1) % 64
    swapped = jnp.where(lane < 32, pltpu.roll(values, 96, 1), pltpu.roll(values, 32, 1))
    return values * cosine + swapped * sine_part


def rope_forward_kernel(groups, qkv_ref, scale_ref, cos_ref, sin_ref, q_ref, kv_ref):
    rows = qkv_ref.shape[0]
    scale = scale_ref[...]
    cosine, sine_part = cos_ref[...], sin_ref[...]
    lane = lax.broadcasted_iota(jnp.int32, (rows, 128), 1)
    for head in range(groups):
        part = qkv_ref[:, (head // 2) * 128 : (head // 2) * 128 + 128] * scale
        if head % 2:
            part = pltpu.roll(part, 64, 1)
        turned = rotated(part, cosine, sine_part)
        turned = jnp.where(lane < 64, turned.astype(BF).astype(F32) * (1.0 / math.sqrt(HD)), 0.0)
        q_ref[:, head] = turned.astype(BF).reshape(rows // 64, 64, 128)
    part = qkv_ref[:, groups * 64 : groups * 64 + 128] * scale
    kv_ref[...] = rotated(part, cosine, sine_part).astype(BF)


def rope_backward_kernel(groups, pieces, *refs):
    dq_ref, dkv_refs, (scale_ref, cos_ref, sin_ref, out_ref) = (
        refs[0],
        refs[1 : 1 + pieces],
        refs[1 + pieces :],
    )
    rows = out_ref.shape[0]
    scale = scale_ref[...]
    cosine, sine_part = cos_ref[...], -sin_ref[...]
    lane = lax.broadcasted_iota(jnp.int32, (rows, 128), 1)
    for pair in range(groups // 2):
        first = rotated(dq_ref[:, 2 * pair].reshape(rows, 128), cosine, sine_part)
        second = rotated(dq_ref[:, 2 * pair + 1].reshape(rows, 128), cosine, sine_part)
        both = jnp.where(lane < 64, first, pltpu.roll(second, 64, 1))
        out_ref[:, pair * 128 : pair * 128 + 128] = (
            both * (scale * (1.0 / math.sqrt(HD)))
        ).astype(BF)
    total = dkv_refs[0][...].astype(F32)
    for ref in dkv_refs[1:]:
        total = total + ref[...].astype(F32)
    out_ref[:, groups * 64 : groups * 64 + 128] = (
        rotated(total, cosine, sine_part) * scale
    ).astype(BF)


def sort_keys(pbk_ref, kv_refs, sorted_ref):
    per_piece = kv_refs[0].shape[0] // 64
    for m, kv_ref in enumerate(kv_refs):
        for block in range(per_piece):
            at = pl.multiple_of(pbk_ref[m * per_piece + block] * 64, 64)
            sorted_ref[pl.ds(at, 64), :] = kv_ref[block * 64 : block * 64 + 64, :]


def visible(tile_index, block_pos, rows):
    key_pos = tile_index * TK + lax.broadcasted_iota(jnp.int32, (rows, TK), 1)
    query_pos = block_pos * 64 + lax.broadcasted_iota(jnp.int32, (rows, TK), 0) % 64
    return key_pos <= query_pos


def attention_forward_kernel(groups, pieces, pbq_ref, pbk_ref, q_ref, *refs):
    kv_refs, (mixed_ref, aux_ref, sorted_ref, score_ref) = refs[:pieces], refs[pieces:]
    step = pl.program_id(0)
    rows = groups * 64

    @pl.when(step == 0)
    def _():
        sort_keys(pbk_ref, kv_refs, sorted_ref)

    block_pos = pbq_ref[step]
    tiles = (block_pos * 64) // TK + 1
    queries = q_ref[0].reshape(rows, 128)

    def first_pass(tile_index, maxima):
        keys = sorted_ref[pl.ds(pl.multiple_of(tile_index * TK, TK), TK), :]
        scores = mm_nt(queries, keys)
        scores = jnp.where(visible(tile_index, block_pos, rows), scores, NEG)
        score_ref[tile_index] = scores
        for part in range(TK // 128):
            maxima = jnp.maximum(maxima, scores[:, part * 128 : part * 128 + 128])
        return maxima

    maxima = lax.fori_loop(0, tiles, first_pass, jnp.full((rows, 128), NEG, F32))
    row_max = jnp.max(maxima, axis=1, keepdims=True)

    def second_pass(tile_index, carry):
        totals, accum = carry
        keys = sorted_ref[pl.ds(pl.multiple_of(tile_index * TK, TK), TK), :]
        weights = jnp.exp(score_ref[tile_index] - row_max)
        for part in range(TK // 128):
            totals = totals + weights[:, part * 128 : part * 128 + 128]
        return totals, accum + mm(weights.astype(BF), keys)

    zeros = jnp.zeros((rows, 128), F32)
    totals, accum = lax.fori_loop(0, tiles, second_pass, (zeros, zeros))
    row_total = jnp.sum(totals, axis=1, keepdims=True)
    accum = accum * (1.0 / row_total)
    lane = lax.broadcasted_iota(jnp.int32, (rows, 128), 1)
    aux_ref[0] = jnp.where(lane < 64, row_max + jnp.log(row_total), accum)
    short = lax.broadcasted_iota(jnp.int32, (64, 128), 1)
    for pair in range(groups // 2):
        first = accum[2 * pair * 64 : 2 * pair * 64 + 64]
        second = accum[(2 * pair + 1) * 64 : (2 * pair + 1) * 64 + 64]
        mixed_ref[:, pair * 128 : pair * 128 + 128] = jnp.where(
            short < 64, pltpu.roll(first, 64, 1), second
        ).astype(BF)


def attention_backward_kernel(groups, pieces, pbq_ref, pbk_ref, q_ref, g_ref, aux_ref, *refs):
    kv_refs, dq_ref, dkv_refs = refs[:pieces], refs[pieces], refs[pieces + 1 : 2 * pieces + 1]
    sorted_ref, sum_ref = refs[2 * pieces + 1 :]
    step = pl.program_id(0)
    rows = groups * 64

    @pl.when(step == 0)
    def _():
        sort_keys(pbk_ref, kv_refs, sorted_ref)
        sum_ref[...] = jnp.zeros(sum_ref.shape, F32)

    block_pos = pbq_ref[step]
    tiles = (block_pos * 64) // TK + 1
    queries = q_ref[0].reshape(rows, 128)
    aux = aux_ref[0]
    short = lax.broadcasted_iota(jnp.int32, (64, 128), 1)
    parts = []
    for head in range(groups):
        part = g_ref[:, (head // 2) * 128 : (head // 2) * 128 + 128].astype(F32)
        if head % 2 == 0:
            part = pltpu.roll(part, 64, 1)
        parts.append(jnp.where(short < 64, 0.0, part))
    grads_f = jnp.concatenate(parts, axis=0)
    delta = jnp.sum(grads_f * aux, axis=1, keepdims=True)
    log_total = aux[:, :1]
    grads = grads_f.astype(BF)

    def visit(tile_index, grad_q):
        where_at = pl.ds(pl.multiple_of(tile_index * TK, TK), TK)
        keys = sorted_ref[where_at, :]
        scores = mm_nt(queries, keys)
        scores = jnp.where(visible(tile_index, block_pos, rows), scores - log_total, NEG)
        weights = jnp.exp(scores)
        grad_prob = mm_nt(grads, keys)
        grad_score = (weights * (grad_prob - delta)).astype(BF)
        sum_ref[where_at, :] += mm_tn(grad_score, queries) + mm_tn(weights.astype(BF), grads)
        return grad_q + mm(grad_score, keys)

    grad_q = lax.fori_loop(0, tiles, visit, jnp.zeros((rows, 128), F32))
    dq_ref[0] = grad_q.reshape(groups, 64, 128)

    @pl.when(step == pl.num_programs(0) - 1)
    def _():
        per_piece = dkv_refs[0].shape[0] // 64
        for m, dkv_ref in enumerate(dkv_refs):
            for block in range(per_piece):
                at = pl.multiple_of(pbk_ref[m * per_piece + block] * 64, 64)
                dkv_ref[block * 64 : block * 64 + 64, :] = sum_ref[pl.ds(at, 64), :].astype(BF)


def pick_kernel(ids_ref, x_ref, c_ref, x_out_ref, c_out_ref):
    for j in range(x_out_ref.shape[1] // 128):
        at = pl.multiple_of(ids_ref[j] * 128, 128)
        x_out_ref[:, j * 128 : j * 128 + 128] = x_ref[:, pl.ds(at, 128)]
        c_out_ref[:, j * 128 : j * 128 + 128] = c_ref[:, pl.ds(at, 128)]


def spread_kernel(ids_ref, own_ref, other_ref, out_ref, both_ref):
    both_ref[0] = own_ref[...]
    both_ref[1] = other_ref[...]
    for j in range(out_ref.shape[1] // 128):
        at = pl.multiple_of(ids_ref[1, j] * 128, 128)
        out_ref[:, j * 128 : j * 128 + 128] = both_ref[ids_ref[0, j], :, pl.ds(at, 128)]


def through(copies_in, copies_out):
    for copy in copies_in:
        copy.start()
    for copy_in, copy_out in zip(copies_in, copies_out):
        copy_in.wait()
        copy_out.start()
    for copy in copies_out:
        copy.wait()


def place_kernel(na, *refs):
    index_ref, pieces, out_ref = refs[0], refs[1 : 1 + na], refs[1 + na]
    buffer_ref, sems_in, sems_out = refs[2 + na :]
    rows = pieces[0].shape[0]
    copies_in, copies_out = [], []
    for k in range(na):
        at = pl.multiple_of((index_ref[0] ^ k) * rows, rows)
        copies_in.append(pltpu.make_async_copy(pieces[k], buffer_ref.at[k], sems_in.at[k]))
        copies_out.append(
            pltpu.make_async_copy(buffer_ref.at[k], out_ref.at[pl.ds(at, rows), :], sems_out.at[k])
        )
    through(copies_in, copies_out)


def join_kernel(starts, *refs):
    out_ref, buffer_ref, sems_in, sems_out = refs[-4:]
    at = 0
    copies_in, copies_out = [], []
    for n, (start, rows, ref) in enumerate(zip(*starts, refs[:-4])):
        part = buffer_ref.at[at : at + rows, :]
        copies_in.append(
            pltpu.make_async_copy(ref.at[start : start + rows, :], part, sems_in.at[n])
        )
        copies_out.append(
            pltpu.make_async_copy(part, out_ref.at[at : at + rows, :], sems_out.at[n])
        )
        at += rows
    through(copies_in, copies_out)


def pick(ids, x, c):
    smem = pl.BlockSpec(memory_space=pltpu.SMEM)
    vmem = pl.BlockSpec(memory_space=pltpu.VMEM)
    shape = jax.ShapeDtypeStruct((x.shape[0], x.shape[1] // 2), x.dtype)
    return pl.pallas_call(
        pick_kernel,
        in_specs=[smem, vmem, vmem],
        out_specs=[vmem, vmem],
        out_shape=[shape, shape],
        name="pick",
    )(ids, x, c)


def spread(ids, own, other):
    rows, columns = own.shape
    smem = pl.BlockSpec(memory_space=pltpu.SMEM)
    vmem = pl.BlockSpec(memory_space=pltpu.VMEM)
    return pl.pallas_call(
        spread_kernel,
        in_specs=[smem, vmem, vmem],
        out_specs=vmem,
        out_shape=jax.ShapeDtypeStruct((rows, 2 * columns), own.dtype),
        scratch_shapes=[pltpu.VMEM((2, rows, columns), own.dtype)],
        name="spread",
    )(ids, own, other)


def place(index, pieces):
    rows, columns = pieces[0].shape
    smem = pl.BlockSpec(memory_space=pltpu.SMEM)
    hbm = pl.BlockSpec(memory_space=pl.ANY)
    return pl.pallas_call(
        functools.partial(place_kernel, len(pieces)),
        in_specs=[smem] + [hbm] * len(pieces),
        out_specs=hbm,
        out_shape=jax.ShapeDtypeStruct((len(pieces) * rows, columns), pieces[0].dtype),
        scratch_shapes=[
            pltpu.VMEM((len(pieces), rows, columns), pieces[0].dtype),
            pltpu.SemaphoreType.DMA((len(pieces),)),
            pltpu.SemaphoreType.DMA((len(pieces),)),
        ],
        name="place",
    )(index, *pieces)


def join(parts):
    starts = tuple(p[1] for p in parts), tuple(p[2] for p in parts)
    shape = jax.ShapeDtypeStruct((sum(starts[1]), parts[0][0].shape[1]), parts[0][0].dtype)
    hbm = pl.BlockSpec(memory_space=pl.ANY)
    return pl.pallas_call(
        functools.partial(join_kernel, starts),
        in_specs=[hbm] * len(parts),
        out_specs=hbm,
        out_shape=shape,
        scratch_shapes=[
            pltpu.VMEM(shape.shape, shape.dtype),
            pltpu.SemaphoreType.DMA((len(parts),)),
            pltpu.SemaphoreType.DMA((len(parts),)),
        ],
        name="join",
    )(*[p[0] for p in parts])


def rope_forward(qkv, scale, cosine, sine_part, groups):
    rows = qkv.shape[0]
    return pl.pallas_call(
        functools.partial(rope_forward_kernel, groups),
        out_shape=(
            jax.ShapeDtypeStruct((rows // 64, groups, 64, 128), BF),
            jax.ShapeDtypeStruct((rows, 128), BF),
        ),
        name="rope_forward",
    )(qkv, scale, cosine, sine_part)


def rope_backward(dq, dkv_pieces, scale, cosine, sine_part, groups):
    rows = scale.shape[0]
    return pl.pallas_call(
        functools.partial(rope_backward_kernel, groups, len(dkv_pieces)),
        out_shape=jax.ShapeDtypeStruct((rows, groups * 64 + 128), BF),
        name="rope_backward",
    )(dq, *dkv_pieces, scale, cosine, sine_part)


def attention_forward(queries, kv, pbq, pbk):
    blocks, groups = queries.shape[:2]
    piece = kv[0].shape[0]
    keys = len(kv) * piece
    smem = pl.BlockSpec(memory_space=pltpu.SMEM)
    return pl.pallas_call(
        functools.partial(attention_forward_kernel, groups, len(kv)),
        grid=(blocks,),
        in_specs=[
            smem,
            smem,
            pl.BlockSpec((1, groups, 64, 128), lambda i: (i, 0, 0, 0)),
        ]
        + [pl.BlockSpec((piece, 128), lambda i: (0, 0))] * len(kv),
        out_specs=(
            pl.BlockSpec((64, groups * 64), lambda i: (i, 0)),
            pl.BlockSpec((1, groups * 64, 128), lambda i: (i, 0, 0)),
        ),
        out_shape=(
            jax.ShapeDtypeStruct((blocks * 64, groups * 64), BF),
            jax.ShapeDtypeStruct((blocks, groups * 64, 128), F32),
        ),
        scratch_shapes=[
            pltpu.VMEM((keys, 128), BF),
            pltpu.VMEM((keys // TK, groups * 64, TK), F32),
        ],
        name="attention_forward",
    )(pbq, pbk, queries, *kv)


def attention_backward(queries, grads, aux, kv, pbq, pbk):
    blocks, groups = queries.shape[:2]
    piece = kv[0].shape[0]
    keys = len(kv) * piece
    piece_spec = pl.BlockSpec((piece, 128), lambda i: (0, 0))
    smem = pl.BlockSpec(memory_space=pltpu.SMEM)
    return pl.pallas_call(
        functools.partial(attention_backward_kernel, groups, len(kv)),
        grid=(blocks,),
        in_specs=[
            smem,
            smem,
            pl.BlockSpec((1, groups, 64, 128), lambda i: (i, 0, 0, 0)),
            pl.BlockSpec((64, groups * 64), lambda i: (i, 0)),
            pl.BlockSpec((1, groups * 64, 128), lambda i: (i, 0, 0)),
        ]
        + [piece_spec] * len(kv),
        out_specs=[pl.BlockSpec((1, groups, 64, 128), lambda i: (i, 0, 0, 0))]
        + [piece_spec] * len(kv),
        out_shape=[jax.ShapeDtypeStruct((blocks, groups, 64, 128), F32)]
        + [jax.ShapeDtypeStruct((piece, 128), BF)] * len(kv),
        scratch_shapes=[pltpu.VMEM((keys, 128), BF), pltpu.VMEM((keys, 128), F32)],
        name="attention_backward",
    )(pbq, pbk, queries, grads, aux, *kv)


def per_device(
    tokens,
    gain_attention,
    query_weight,
    key_weight,
    value_weight,
    output_weight,
    gain_feedforward,
    gate_weight,
    up_weight,
    down_weight,
    cotangent,
):
    shard_rows, width = tokens.shape
    n_ctx = lax.axis_size("ctx")
    ctx_index = lax.axis_index("ctx")
    core = lax.axis_index("tp")
    na = key_weight.shape[1] // HD
    nb = n_ctx // na
    a_index, b_index = ctx_index // nb, ctx_index % nb
    a_array = a_index.astype(jnp.int32)[None]
    d_rows = width // n_ctx
    half = width // 2
    group_rows = na * shard_rows
    groups = query_weight.shape[1] // key_weight.shape[1]
    chunk = na * d_rows
    quarter = chunk // 2
    square = nb == 4 and na == 4
    gain_a = gain_attention.astype(F32)[:, None]
    gain_m = gain_feedforward.astype(F32)[:, None]

    def swap_a(value, k):
        return lax.ppermute(value, "ctx", [(i, i ^ (k * nb)) for i in range(n_ctx)])

    def swap_b(value, m):
        return lax.ppermute(value, "ctx", [(i, i ^ m) for i in range(n_ctx)])

    def swap_core(value):
        return lax.ppermute(value, "tp", [(0, 1), (1, 0)])

    if square:
        halves = [(0, 0), (0, 1), (1, 0), (3, 0), (2, 1), (3, 1), (2, 0), (1, 1)]
        blocks_of = [(m, 2 * n + j) for m, n in halves for j in range(2)]
    else:
        blocks_of = [(m, a) for m in range(nb) for a in range(na)]
    count = n_ctx // 2
    block_m = jnp.array([m for m, _ in blocks_of], jnp.int32)
    block_a = jnp.array([a for _, a in blocks_of], jnp.int32)
    natural_ids = block_a * nb + (block_m ^ b_index)
    half_ids = lax.dynamic_slice_in_dim(natural_ids, core * count, count)
    place_of = [[blocks_of.index((m, a)) for m in range(nb)] for a in range(na)]
    natural_at = jnp.array(place_of, jnp.int32)[
        jnp.arange(n_ctx) // nb, (jnp.arange(n_ctx) % nb) ^ b_index
    ]
    spread_ids = jnp.stack([(natural_at // count) ^ core, natural_at % count])

    def half_features(first, second):
        if d_rows % 128 == 0:
            return pick(half_ids, first, second)
        return [
            jnp.concatenate(
                [
                    lax.dynamic_slice_in_dim(value, half_ids[j] * d_rows, d_rows, 1)
                    for j in range(count)
                ],
                axis=1,
            )
            for value in (first, second)
        ]

    def whole_rows(own, other):
        if d_rows % 128 == 0:
            return spread(spread_ids, own, other)
        both = jnp.concatenate([own, other], axis=1)
        return jnp.concatenate(
            [
                lax.dynamic_slice_in_dim(
                    both, (spread_ids[0, j] * count + spread_ids[1, j]) * d_rows, d_rows, 1
                )
                for j in range(n_ctx)
            ],
            axis=1,
        )

    def both_cores(own, other):
        first = jnp.where(core == 0, own, other)
        second = jnp.where(core == 0, other, own)
        return jnp.concatenate([first, second], axis=1)

    far_k, near_k = na // 2, 1
    row_order = [0, 2, 1, 3]

    def gather_one(own_half):
        return swap_a(own_half, far_k)

    def gather_two(own_half, got):
        two = jnp.concatenate([own_half, got], axis=0)
        return two, swap_a(two, near_k)

    def gather_three(two, got):
        stacked = jnp.concatenate([two, got], axis=0)
        return both_cores(stacked, swap_core(stacked))

    def gather_rows(own_half):
        two, got = gather_two(own_half, gather_one(own_half))
        return gather_three(two, got)

    def reduce_rows(product_of_half):
        sent = product_of_half(1 - core).astype(BF)
        other = swap_core(sent)
        own = product_of_half(core)
        rows = 2 * shard_rows
        near = own[:rows] + other[:rows].astype(F32)
        sent = (own[rows:] + other[rows:].astype(F32)).astype(BF)
        got = swap_a(sent, near_k)
        rows = shard_rows
        sent = (near[rows:] + got[rows:].astype(F32)).astype(BF)
        last = swap_a(sent, far_k)
        return near[:rows] + got[:rows].astype(F32) + last.astype(F32)

    def half_rows(value, which):
        return lax.dynamic_slice_in_dim(value, which * half, half, 0)

    def unit_block(weight, which):
        size = weight.shape[1] // na
        return lax.dynamic_slice_in_dim(weight, which * size, size, 1)

    def gained(weight, gain):
        return (weight.astype(F32) * gain).astype(BF)

    def gather_weight(blocks):
        pieces = [blocks(a_index)]
        for k in range(1, na):
            pieces.append(swap_a(blocks(a_index ^ k), k))
        own = place(a_array, pieces)
        if not square:
            return jnp.concatenate([own] + [swap_b(own, m) for m in range(1, nb)], axis=0)
        one, two = swap_b(own, 1), swap_b(own, 2)
        three_0 = swap_b(one[:quarter], 2)
        three_1 = swap_b(two[quarter:], 1)
        return join(
            [
                (own, 0, chunk),
                (one, 0, quarter),
                (three_0, 0, quarter),
                (two, quarter, quarter),
                (three_1, 0, quarter),
                (two, 0, quarter),
                (one, quarter, quarter),
            ]
        )

    def scatter_grad(left, right):
        def product(start, stop):
            return mm_tn(left[:, start * quarter : stop * quarter], right)

        if square:
            got = [swap_b(product(2, 4).astype(BF), 1), swap_b(product(4, 6).astype(BF), 2)]
            own, rest = product(0, 2), product(6, 8)
            parts = []
            for n in range(2):
                at = slice(n * quarter, (n + 1) * quarter)
                sent = (rest[at] + got[n][quarter:].astype(F32)).astype(BF)
                last = swap_b(sent, 2 - n)
                parts.append(own[at] + got[n][:quarter].astype(F32) + last.astype(F32))
            summed = jnp.concatenate(parts, axis=0).astype(BF)
        else:
            summed = product(0, 2)
            for m in range(1, nb):
                got = swap_b(product(2 * m, 2 * m + 2).astype(BF), m)
                summed = summed + got.astype(F32)
            summed = summed.astype(BF)
        blocks = summed.reshape(na, d_rows, summed.shape[1])
        pieces = []
        for k in range(na):
            piece = lax.dynamic_slice_in_dim(blocks, a_index ^ k, 1, 0)[0]
            pieces.append(piece if k == 0 else swap_a(piece, k))
        return pieces

    def qkv_blocks(which):
        return jnp.concatenate(
            [
                gained(unit_block(weight, which), gain_a)
                for weight in (query_weight, key_weight, value_weight)
            ],
            axis=1,
        )

    x_half, c_half = half_features(tokens, cotangent)
    x_all = gather_rows(x_half)
    c_all = gather_rows(c_half)
    qkv_all = gather_weight(qkv_blocks)
    output_all = gather_weight(lambda which: unit_block(output_weight, which))
    gate_all = gather_weight(lambda which: gained(unit_block(gate_weight, which), gain_m))
    up_all = gather_weight(lambda which: gained(unit_block(up_weight, which), gain_m))
    down_all = gather_weight(lambda which: unit_block(down_weight, which))

    k_shards = ctx_index ^ (jnp.array(row_order, jnp.int32) * nb)
    m_shards = k_shards[None, :] ^ jnp.arange(nb, dtype=jnp.int32)[:, None]
    pbq = jnp.stack([k_shards, 2 * n_ctx - 1 - k_shards], axis=1).reshape(na * 2)
    pbk = jnp.stack([m_shards, 2 * n_ctx - 1 - m_shards], axis=2).reshape(nb * na * 2)
    block_rows = shard_rows // 2
    positions = (
        pbq[:, None] * block_rows + jnp.arange(block_rows, dtype=jnp.int32)[None, :]
    ).reshape(group_rows)
    frequency = jnp.exp(
        -jnp.arange(HD // 2, dtype=F32) * (2.0 * math.log(500000.0) / HD)
    )
    angles = positions.astype(F32)[:, None] * frequency[None, :]
    cos_part, sin_part = jnp.cos(angles), jnp.sin(angles)
    cosine = jnp.concatenate(
        [cos_part, cos_part, jnp.ones((group_rows, HD), F32)], axis=1
    )
    sine_part = jnp.concatenate(
        [-sin_part, sin_part, jnp.zeros((group_rows, HD), F32)], axis=1
    )

    x_f = x_all.astype(F32)
    r1 = lax.rsqrt(jnp.mean(x_f * x_f, axis=1, keepdims=True) + EPSILON)
    qkv = mm(x_all, qkv_all)
    queries, kv_own = rope_forward(qkv, r1, cosine, sine_part, groups)
    kv = [kv_own] + [swap_b(kv_own, m) for m in range(1, nb)]
    mixed, aux = attention_forward(queries, kv, pbq, pbk)
    branch = reduce_rows(lambda which: mm_nt(mixed, half_rows(output_all, which)))
    middle = x_half.astype(F32) + branch

    middle_all = gather_rows(middle.astype(BF))
    middle_f = middle_all.astype(F32)
    r2 = lax.rsqrt(jnp.mean(middle_f * middle_f, axis=1, keepdims=True) + EPSILON)
    gate_pre = mm(middle_all, gate_all) * r2
    upward = mm(middle_all, up_all) * r2
    sigmoid_gate = jax.nn.sigmoid(gate_pre)
    silu_gate = gate_pre * sigmoid_gate
    hidden = (silu_gate * upward).astype(BF)

    grad_hidden = mm(c_all, down_all)
    grad_gate_pre = (
        grad_hidden * upward * sigmoid_gate * (1.0 + gate_pre * (1.0 - sigmoid_gate)) * r2
    ).astype(BF)
    grad_upward = (grad_hidden * silu_gate * r2).astype(BF)
    grad_ff = reduce_rows(
        lambda which: mm_nt(grad_gate_pre, half_rows(gate_all, which))
        + mm_nt(grad_upward, half_rows(up_all, which)),
    )
    down_pieces = scatter_grad(c_all, hidden)
    gate_pieces = scatter_grad(middle_all, grad_gate_pre)
    up_pieces = scatter_grad(middle_all, grad_upward)

    def norm_backward(values, inverse, grad_scaled):
        part = jnp.sum(grad_scaled * values, axis=1)
        mean = ((part + swap_core(part)) * (1.0 / width))[:, None]
        return grad_scaled - values * (inverse * inverse) * mean

    grad_middle = c_half.astype(F32) + norm_backward(middle, r2[:shard_rows], grad_ff)
    branch_all = gather_rows(grad_middle.astype(BF))
    ff_out = reduce_rows(lambda which: mm_nt(hidden, half_rows(down_all, which)))

    grad_mixed = mm(branch_all, output_all).astype(BF)
    dq, *dkv = attention_backward(queries, grad_mixed, aux, kv, pbq, pbk)
    dkv = [dkv[0]] + [swap_b(dkv[m], m) for m in range(1, nb)]
    output_pieces = scatter_grad(branch_all, mixed)
    grad_qkv = rope_backward(dq, dkv, r1, cosine, sine_part, groups)
    grad_in = reduce_rows(lambda which: mm_nt(grad_qkv, half_rows(qkv_all, which)))
    qkv_pieces = scatter_grad(x_all, grad_qkv)
    tokens_half = grad_middle + norm_backward(x_half.astype(F32), r1[:shard_rows], grad_in)
    grad_tokens = whole_rows(tokens_half, swap_core(tokens_half))

    units = gate_all.shape[1]
    (grad_down,) = finish(a_array, down_pieces, gain_m, [], [units])
    grad_gate, gate_dot = finish(a_array, gate_pieces, gain_m, [gate_weight], [units])
    layer_half = middle + ff_out
    layer_output = whole_rows(layer_half, swap_core(layer_half))
    grad_up, up_dot = finish(a_array, up_pieces, gain_m, [up_weight], [units])
    grad_query, grad_key, grad_value, part_a = finish(
        a_array,
        qkv_pieces,
        gain_a,
        [query_weight, key_weight, value_weight],
        [groups * HD, HD, HD],
    )
    dots = jnp.concatenate([part_a[:, 0], gate_dot[:, 0] + up_dot[:, 0]])
    dots = dots + swap_core(dots)
    (grad_output,) = finish(a_array, output_pieces, gain_a, [], [groups * HD])
    return (
        layer_output,
        grad_tokens,
        dots[:d_rows],
        grad_query,
        grad_key,
        grad_value,
        grad_output,
        dots[d_rows:],
        grad_gate,
        grad_up,
        grad_down,
    )


def solution(mesh):
    rows, units = P("ctx", None), P("ctx", "tp")
    in_specs = (rows, P("ctx"), units, units, units, units, P("ctx"), units, units, units, rows)
    out_specs = (rows, rows, P("ctx"), units, units, units, units, P("ctx"), units, units, units)

    return jax.shard_map(
        per_device, mesh=mesh, in_specs=in_specs, out_specs=out_specs, check_vma=False
    )
```
